32 devices in a mesh: ctx: 8 (over z, y), exp: 4 (over x, core).
Axes of the slice: x: 2, y: 2, z: 4, core: 2. Of those that a mesh axis runs over, the one named last changes fastest.
Arguments:
- queries: bfloat16 [1024, 4096], P('ctx', 'exp'), may hold values from -0.5 to 0.5
- attn_keys: bfloat16 [1024, 4096], P('ctx', 'exp'), may hold values from -0.5 to 0.5
- attn_values: bfloat16 [1024, 4096], P('ctx', 'exp'), may hold values from -3 to 3
- out_grad: bfloat16 [1024, 4096], P('ctx', 'exp'), may hold values from -0.75 to 0.75
- log_decay: float32 [1024, 32], P('ctx', 'exp'), may hold values from -1 to 0
- moe_input: bfloat16 [1024, 3072], P(('ctx', 'exp')), may hold values from -6 to 6
- routes: int32 [1024, 2], P(('ctx', 'exp')), may hold values from 0 to 7, all different within a row; in each aligned block of 32 rows (0 to 31, 32 to 63, ...) at most 16 rows name the same one
- route_weight: float32 [1024, 2], P(('ctx', 'exp')), may hold values from 0.25 to 1
- w_gate: bfloat16 [8, 9216, 3072], P('exp', 'ctx'), may hold values from -0.109375 to 0.109375
- w_up: bfloat16 [8, 9216, 3072], P('exp', 'ctx'), may hold values from -0.109375 to 0.109375
- w_down: bfloat16 [8, 9216, 3072], P('exp', 'ctx'), may hold values from -0.0625 to 0.0625
Outputs:
- attn_out: bfloat16 [1024, 4096], P('ctx', 'exp')
- grad_q: bfloat16 [1024, 4096], P('ctx', 'exp')
- grad_k: bfloat16 [1024, 4096], P('ctx', 'exp')
- derivative_wrt_entries: bfloat16 [1024, 4096], P('ctx', 'exp')
- moe_out: bfloat16 [1024, 3072], P(('ctx', 'exp'))
The draws below stay inside these ranges and needn't reach their ends.
Inputs may be any that keep to these rules, and one draw needn't show every extreme that they name: `routes`: in the rows of one device no expert is named more than 16 times; each row names two different experts.
All inputs are finite; a program needn't handle non-finite values.
Results may differ from the reference program's by a relative error of at most 0.025.
Values may be sent and summed in bfloat16 or wider, within the bound.
No kernel may reach another device: no remote copies, remote signals or barrier semaphores. Data moves between devices by JAX's collectives and lax.ppermute only.
A program may use at most 128 MiB of HBM per device.

```python
import math
import jax
import jax.numpy as jnp
import numpy as np
from jax import lax

D = 3072
HEADS = 32
HDIM = 128
EXPERTS = 8
FF = 9216
TOK_DEV = 128
MTOK_DEV = 32
CAP = 16
PACKED_LENGTH = 1024
MTOKENS = 1024
FSLICE = 1152
N_CTX = 8
N_EXP = 4


def draw_log_decay(key, part):
    concurrent_tracks = jax.random.split(key, 6)
    share = 0.5
    quick = jax.random.uniform(concurrent_tracks[0], (HEADS,)) < share
    memory_span = jax.random.uniform(concurrent_tracks[1], (HEADS,), minval=30.0, maxval=50.0)
    rate = jnp.where(quick, 2.302585 / memory_span, 0.1 / PACKED_LENGTH)
    block_count = PACKED_LENGTH // TOK_DEV
    block_factor = jnp.exp(jax.random.uniform(concurrent_tracks[2], (block_count, HEADS), minval=-0.5, maxval=0.5))
    jitter = jax.random.uniform(concurrent_tracks[3], (PACKED_LENGTH, HEADS), minval=0.5, maxval=1.5)
    baseline = -rate[None, :] * jnp.repeat(block_factor, TOK_DEV, axis=0) * jitter
    position_groupings = jax.random.randint(concurrent_tracks[4], (3,), 0, PACKED_LENGTH)
    dropped_flag = jnp.any(jnp.arange(PACKED_LENGTH)[:, None] == position_groupings[None, :], axis=1)
    losses = jnp.log(jax.random.uniform(concurrent_tracks[5], (PACKED_LENGTH, HEADS), minval=0.5, maxval=0.8))
    return jnp.where(dropped_flag[:, None], baseline + losses, baseline).astype(jnp.float32)


def block_levels(key, dims, cuts, smallest, top_value):
    gain, own = 1.0, jax.random.fold_in(key, 6)
    for dim, blocks in cuts:
        heights = jnp.exp(jax.random.uniform(jax.random.fold_in(own, dim), (blocks,), jnp.float32, smallest / len(cuts), top_value / len(cuts)))
        gain = gain * jnp.repeat(heights, dims[dim] // blocks).reshape([-1 if axis == dim else 1 for axis in range(len(dims))])
    return gain


def shared_out(own_key, own, number, rows, number_of, top, limit, slope):
    sequence = jax.random.permutation(own_key, number_of)
    packed, ordinary = shares(number_of, rows * top, limit, slope, True), shares(number_of, rows * top, limit, slope, False)
    places = jnp.arange(number_of)

    def named(tallies, turn):
        used = int((tallies > 0).sum())
        fixed = max(1, used // 4)
        shifted = fixed + (places - fixed + turn * (used - fixed)) % max(1, number_of - fixed)
        return jnp.zeros((number_of,), jnp.int32).at[sequence[jnp.where(places < fixed, places, shifted)]].set(jnp.asarray(tallies, jnp.int32))

    tallies = jnp.where(number % 4 == 0, named(packed, number // 4), named(ordinary, number - number // 4 - 1))
    mixed = jax.random.permutation(jax.random.fold_in(own, 3), number_of)
    source_of, receiver = mixed[0:number_of // 2 * 2:2], mixed[1:number_of // 2 * 2:2]
    slack = jnp.minimum(tallies[source_of] - 1, limit - tallies[receiver]) // 2
    slack = jnp.where((source_of == sequence[0]) | (receiver == sequence[0]) | (tallies[receiver] == 0), 0, jnp.maximum(slack, 0))
    shifted = jax.random.randint(jax.random.fold_in(own, 4), (number_of // 2,), 0, 1 << 20) % (slack + 1)
    tallies = tallies.at[source_of].add(-shifted).at[receiver].add(shifted)
    members = jnp.searchsorted(jnp.cumsum(tallies), jnp.arange(rows * top), side="right").astype(jnp.int32)
    listing = members.reshape(top, rows).T
    listing = listing[jax.random.permutation(jax.random.fold_in(own, 1), rows)]
    turn = jax.random.randint(jax.random.fold_in(own, 2), (rows, 1), 0, top)
    return jnp.take_along_axis(listing, (jnp.arange(top)[None, :] + turn) % top, axis=1)


def shares(amount, total, most, skew, full):
    loads = [(1 << 20) // math.isqrt(standing ** skew) + 1 for standing in range(1, amount + 1)]
    largest = most if full else min(most, max(-(-total // amount), total * loads[0] // sum(loads)))
    least = 1 if total - largest >= amount - 1 else 0
    counts, spare = [largest] + [least] * (amount - 1), total - largest - least * (amount - 1)
    while spare > 0:
        movable = [i for i in range(1, amount) if counts[i] < largest] or [i for i in range(1, amount) if counts[i] < most]
        pool, remaining = sum([loads[i] for i in movable]), spare
        for i in movable:
            more = min(most - counts[i], max(1, remaining * loads[i] // pool), spare)
            counts[i] = counts[i] + more
            spare = spare - more
    return np.array(counts)


def scatter_about(key, extent, scale, most, cuts=(), kind=jnp.bfloat16):
    drawn = scale * jax.random.normal(key, extent, jnp.float32)
    if cuts:
        drawn = drawn * block_levels(key, extent, cuts, -0.22, 0.18)
    return jnp.clip(drawn, -most, most).astype(kind)


def setup_inputs(seed: int = 0) -> dict:
    splits = jax.random.split(jax.random.key(seed), 12)
    queries = scatter_about(splits[0], (PACKED_LENGTH, HEADS * HDIM), HDIM ** -0.5, 0.5, ((0, 8), (1, 4)))
    attn_keys = scatter_about(splits[1], (PACKED_LENGTH, HEADS * HDIM), TOK_DEV ** -0.5, 0.5, ((0, 8), (1, 4)))
    attn_values = scatter_about(splits[2], (PACKED_LENGTH, HEADS * HDIM), 0.5, 3.0, ((0, 8), (1, 4)))
    out_grad = scatter_about(splits[3], (PACKED_LENGTH, HEADS * HDIM), 0.125, 0.75, ((0, 8), (1, 4)))
    log_decay = draw_log_decay(jax.random.fold_in(splits[11], 71), 0)
    moe_input = scatter_about(splits[5], (MTOKENS, D), 1.0, 6.0, ((0, 32),))
    routes_keys = jax.random.split(jax.random.fold_in(splits[6], 1), MTOKENS // MTOK_DEV)
    routes_turns = jax.random.permutation(jax.random.fold_in(splits[6], 3), MTOKENS // MTOK_DEV)
    routes = jax.vmap(lambda own, number: shared_out(jax.random.fold_in(splits[6], 2), own, number, MTOK_DEV, EXPERTS, 2, CAP, 2))(routes_keys, routes_turns).reshape((MTOKENS, 2))
    route_weight = jnp.clip(0.25 + 0.75 * jax.random.uniform(splits[7], (MTOKENS, 2), jnp.float32) ** block_levels(splits[7], (MTOKENS, 2), ((0, 32),), -0.2, 0.2), 0.25, 1.0)
    w_gate = scatter_about(splits[8], (EXPERTS, FF, D), D ** -0.5, 0.109375, ((0, 4), (1, 8)))
    w_up = scatter_about(splits[9], (EXPERTS, FF, D), D ** -0.5, 0.109375, ((0, 4), (1, 8)))
    w_down = scatter_about(splits[10], (EXPERTS, FF, D), FF ** -0.5, 0.0625, ((0, 4), (1, 8)))
    return {"queries": queries, "attn_keys": attn_keys, "attn_values": attn_values, "out_grad": out_grad, "log_decay": log_decay, "moe_input": moe_input, "routes": routes, "route_weight": route_weight, "w_gate": w_gate, "w_up": w_up, "w_down": w_down}


def prepare(queries, attn_keys, attn_values, out_grad, log_decay):
    length = queries.shape[0]
    heads = log_decay.shape[1]
    width = queries.shape[1] // heads
    shaped = (length, heads, width)
    full_queries = queries.astype(jnp.float32).reshape(shaped)
    full_keys = attn_keys.astype(jnp.float32).reshape(shaped)
    full_values = attn_values.astype(jnp.float32).reshape(shaped)
    full_gradient = out_grad.astype(jnp.float32).reshape(shaped)
    cum_decay = jnp.cumsum(log_decay, axis=0)
    total = cum_decay[length - 1]
    position = jnp.arange(length, dtype=jnp.int32)
    causal = (position[:, None] >= position[None, :])[None]
    spread = cum_decay.T[:, :, None] - cum_decay.T[:, None, :]
    block_weight = jnp.where(causal, jnp.exp(jnp.where(causal, spread, jnp.float32(0.0))), jnp.float32(0.0))
    rising_edge = jnp.exp(cum_decay)[:, :, None]
    falling_edge = jnp.exp(total[None, :] - cum_decay)[:, :, None]
    return full_queries, full_keys, full_values, full_gradient, total, block_weight, rising_edge, falling_edge


def summaries(queries, attn_keys, attn_values, out_grad, log_decay):
    full_queries, full_keys, full_values, full_gradient, total, block_weight, rising_edge, falling_edge = prepare(queries, attn_keys, attn_values, out_grad, log_decay)
    running_block_state = jnp.einsum('mly,mlf->lyf', full_keys * falling_edge, full_values, precision=lax.Precision.HIGHEST)
    state_gradient = jnp.einsum('nbd,nbw->bdw', full_queries * rising_edge, full_gradient, precision=lax.Precision.HIGHEST)
    return jnp.exp(total), running_block_state, state_gradient


def finish(queries, attn_keys, attn_values, out_grad, log_decay, prior_memory_matrix, following_state):
    full_queries, full_keys, full_values, full_gradient, total, block_weight, rising_edge, falling_edge = prepare(queries, attn_keys, attn_values, out_grad, log_decay)
    length = queries.shape[0]
    scores = jnp.einsum('thd,shd->hts', full_queries, full_keys)
    attention_result = (scores * block_weight).astype(jnp.bfloat16).astype(jnp.float32)
    layer_output = jnp.einsum('pgm,mpo->gpo', attention_result, full_values) + jnp.einsum('bip,ipu->biu', full_queries * rising_edge, prior_memory_matrix, precision=lax.Precision.HIGHEST)
    dscores = jnp.einsum('thd,shd->hts', full_gradient, full_values)
    weight_gradient = (dscores * block_weight).astype(jnp.bfloat16).astype(jnp.float32)
    query_gradient = jnp.einsum('pgm,mpo->gpo', weight_gradient, full_keys) + jnp.einsum('pig,ijg->pij', full_gradient * rising_edge, prior_memory_matrix, precision=lax.Precision.HIGHEST)
    key_gradient = jnp.einsum('nkg,knv->gnv', weight_gradient, full_queries) + falling_edge * jnp.einsum('jnr,nbr->jnb', full_values, following_state, precision=lax.Precision.HIGHEST)
    value_gradient = jnp.einsum('nkg,knv->gnv', attention_result, full_gradient) + falling_edge * jnp.einsum('umj,mje->ume', full_keys, following_state, precision=lax.Precision.HIGHEST)
    flat_shape = (length, queries.shape[1])
    return (layer_output.reshape(flat_shape).astype(jnp.bfloat16), query_gradient.reshape(flat_shape).astype(jnp.bfloat16),
            key_gradient.reshape(flat_shape).astype(jnp.bfloat16), value_gradient.reshape(flat_shape).astype(jnp.bfloat16))


def route_tables(routes, route_weight, experts, capacity):
    row_count = routes.shape[0]
    flat_routes = routes.reshape(row_count * 2)
    one_hot = (flat_routes[:, None] == jnp.arange(experts, dtype=jnp.int32)[None, :]).astype(jnp.int32)
    earlier_count = jnp.cumsum(one_hot, axis=0) - one_hot
    slot_index = jnp.sum(earlier_count * one_hot, axis=1)
    target = flat_routes * capacity + slot_index
    member = (jnp.arange(experts * capacity, dtype=jnp.int32)[:, None] == target[None, :]).astype(jnp.float32)
    picker = member.reshape(experts * capacity, row_count, 2).sum(axis=2)
    merge_lookup = (member * route_weight.reshape(row_count * 2)[None, :]).reshape(experts * capacity, row_count, 2).sum(axis=2)
    return picker, merge_lookup


def expert_apply(rows, gate_matrix, up_matrix, down_matrix):
    gate_value = jnp.dot(rows, gate_matrix.T, preferred_element_type=jnp.float32)
    up_value = jnp.dot(rows, up_matrix.T, preferred_element_type=jnp.float32)
    hidden = (jax.nn.silu(gate_value) * up_value).astype(jnp.bfloat16)

    def add_slice(running, index):
        start = (index * FSLICE).astype(jnp.int32)
        partial_sum = jnp.dot(lax.dynamic_slice_in_dim(hidden, start, FSLICE, 1), lax.dynamic_slice_in_dim(down_matrix, start, FSLICE, 0), preferred_element_type=jnp.float32)
        partial_sum = lax.optimization_barrier(partial_sum.astype(jnp.bfloat16))
        return running + partial_sum.astype(jnp.float32), None

    running, _ = lax.scan(add_slice, jnp.zeros((rows.shape[0], D), jnp.float32), jnp.arange(N_CTX, dtype=jnp.int32))
    return running.astype(jnp.bfloat16)


def reference(queries, attn_keys, attn_values, out_grad, log_decay, moe_input, routes, route_weight, w_gate, w_up, w_down):
    def blocked(array):
        return array.reshape(N_CTX, TOK_DEV, array.shape[1])

    pieces = (blocked(queries), blocked(attn_keys), blocked(attn_values), blocked(out_grad), blocked(log_decay))
    growth, running_block_state, state_gradient = lax.map(lambda items: summaries(*items), pieces)

    def carry_step(carry, item):
        rate, state = item
        return rate[:, None, None] * carry + state, carry

    start = jnp.zeros(running_block_state.shape[1:], jnp.float32)
    _, prior_memory_matrix = lax.scan(carry_step, start, (growth, running_block_state))
    _, following_state = lax.scan(carry_step, start, (growth, state_gradient), reverse=True)
    results = lax.map(lambda items: finish(*items), pieces + (prior_memory_matrix, following_state))
    attn_out, grad_q, grad_k, derivative_wrt_entries = [item.reshape(PACKED_LENGTH, queries.shape[1]) for item in results]

    device_count = N_CTX * N_EXP
    token_blocks = moe_input.reshape(device_count, MTOK_DEV, D)
    picker, merge_lookup = jax.vmap(lambda rows, weights: route_tables(rows, weights, EXPERTS, CAP))(routes.reshape(device_count, MTOK_DEV, 2), route_weight.reshape(device_count, MTOK_DEV, 2))
    buffers = jnp.einsum('bsm,bmd->bsd', picker, token_blocks.astype(jnp.float32)).astype(jnp.bfloat16)
    buffers = buffers.reshape(device_count, EXPERTS, CAP, D)

    def one_expert(index):
        rows = lax.dynamic_index_in_dim(buffers, index, 1, keepdims=False).reshape(device_count * CAP, D)
        return expert_apply(rows, w_gate[index], w_up[index], w_down[index])

    outputs = lax.map(one_expert, jnp.arange(EXPERTS, dtype=jnp.int32))
    outputs = outputs.reshape(EXPERTS, device_count, CAP, D).transpose(1, 0, 2, 3).reshape(device_count, EXPERTS * CAP, D)
    moe_out = jnp.einsum('bsm,bsd->bmd', merge_lookup, outputs.astype(jnp.float32), precision=lax.Precision.HIGHEST)
    return attn_out, grad_q, grad_k, derivative_wrt_entries, moe_out.reshape(MTOKENS, D).astype(jnp.bfloat16)
```

```python
import jax
import jax.numpy as jnp
from jax import lax
from jax.experimental import pallas as pl
from jax.experimental.pallas import tpu as pltpu
from jax.sharding import PartitionSpec as P

BF = jnp.bfloat16
F32 = jnp.float32
BOTH = ("ctx", "exp")
SIDE = 128


def dg(a, b, ca, cb):
    return lax.dot_general(a, b, (((ca,), (cb,)), ((), ())), preferred_element_type=F32)


def block_of(total, top):
    if total <= top:
        return total
    for b in range(top, 0, -128):
        if total % b == 0:
            return b
    return total


class Plan:
    def __init__(self, n_ctx, n_exp):
        self.n_ctx, self.n_exp = n_ctx, n_exp
        self.cores = 2 if n_exp % 2 == 0 else 1
        nx = n_exp // self.cores
        ny = 1 << (max(0, n_ctx.bit_length() - 1) // 2)
        nz = n_ctx // ny
        bits = lambda axis, n: [(axis, 1 << k) for k in range(n.bit_length() - 1)]
        zs, ys, xs = bits("z", nz)[::-1], bits("y", ny), bits("x", nx)
        self.ny = ny
        self.orders = (zs + xs + ys, ys + zs + xs)
        if not xs:
            self.orders = (zs + ys, zs + ys)
        self.stages = len(self.orders[0])

    def place(self, i):
        c, e = divmod(i, self.n_exp)
        z, y = divmod(c, self.ny)
        x, core = divmod(e, self.cores)
        return {"z": z, "y": y, "x": x, "core": core}

    def index(self, p):
        return (p["z"] * self.ny + p["y"]) * self.n_exp + p["x"] * self.cores + p["core"]

    def flip(self, pick):
        out = []
        for i in range(self.n_ctx * self.n_exp):
            p = self.place(i)
            axis, bit = pick(p)
            p[axis] ^= bit
            out.append((i, self.index(p)))
        return out

    def stage(self, k):
        return self.flip(lambda p: self.orders[p["core"]][k])

    def mate(self):
        return self.flip(lambda p: ("core", 1))

    def block(self, bit):
        return [(i, (c ^ bit) * self.n_exp + e) for i in range(self.n_ctx * self.n_exp) for c, e in [divmod(i, self.n_exp)]]


def send(value, pairs):
    return lax.ppermute(value, BOTH, pairs)


def decays(ld_ref, g_ref):
    n = ld_ref.shape[0]
    low = (lax.broadcasted_iota(jnp.int32, (n, n), 0) >= lax.broadcasted_iota(jnp.int32, (n, n), 1)).astype(F32)
    g_ref[...] = lax.dot_general(
        low, ld_ref[...], (((1,), (0,)), ((), ())), precision=lax.Precision.HIGHEST, preferred_element_type=F32
    )


def column(g_ref, h):
    g = g_ref[...]
    lane = lax.broadcasted_iota(jnp.int32, g.shape, 1)
    return jnp.sum(jnp.where(lane == h, g, 0.0), axis=1, keepdims=True)


def states(q, k, v, d, ld):
    n, heads = ld.shape
    w = q.shape[1] // heads

    def kern(q_r, k_r, v_r, d_r, ld_r, b_r, c_r, g_r):
        h = pl.program_id(0)

        @pl.when(h == 0)
        def _():
            decays(ld_r, g_r)

        g = column(g_r, h)
        fall = jnp.exp(g[n - 1 : n, :] - g)
        b_r[0] = dg((k_r[...].astype(F32) * fall).astype(BF), v_r[...], 0, 0).astype(BF)
        c_r[0] = dg((q_r[...].astype(F32) * jnp.exp(g)).astype(BF), d_r[...], 0, 0).astype(BF)

    tile = pl.BlockSpec((n, w), lambda h: (0, h))
    whole = pl.BlockSpec((n, heads), lambda h: (0, 0))
    out = pl.BlockSpec((1, w, w), lambda h: (h, 0, 0))
    return pl.pallas_call(
        kern,
        grid=(heads,),
        in_specs=[tile] * 4 + [whole],
        out_specs=[out, out],
        out_shape=[jax.ShapeDtypeStruct((heads, w, w), BF)] * 2,
        scratch_shapes=[pltpu.VMEM((n, heads), F32)],
        compiler_params=pltpu.CompilerParams(dimension_semantics=("arbitrary",)),
    )(q, k, v, d, ld)


def finish(q, k, v, d, ld, s, r):
    n, heads = ld.shape
    w = q.shape[1] // heads

    def kern(q_r, k_r, v_r, d_r, ld_r, s_r, r_r, o_r, gq_r, gk_r, gv_r, g_r):
        h = pl.program_id(0)

        @pl.when(h == 0)
        def _():
            decays(ld_r, g_r)

        g = column(g_r, h)
        rise = jnp.exp(g)
        fall = jnp.exp(g[n - 1 : n, :] - g)
        wide = jnp.broadcast_to(g, (n, n))
        causal = lax.broadcasted_iota(jnp.int32, (n, n), 0) >= lax.broadcasted_iota(jnp.int32, (n, n), 1)
        weight = jnp.where(causal, jnp.exp(jnp.where(causal, wide - wide.T, 0.0)), 0.0)
        qh, kh, vh, dh = q_r[...], k_r[...], v_r[...], d_r[...]
        sh, rh = s_r[0].astype(BF), r_r[0].astype(BF)
        attn = (dg(qh, kh, 1, 1) * weight).astype(BF)
        grad = (dg(dh, vh, 1, 1) * weight).astype(BF)
        o_r[...] = (dg(attn, vh, 1, 0) + rise * dg(qh, sh, 1, 0)).astype(BF)
        gq_r[...] = (dg(grad, kh, 1, 0) + rise * dg(dh, sh, 1, 1)).astype(BF)
        gk_r[...] = (dg(grad, qh, 0, 0) + fall * dg(vh, rh, 1, 1)).astype(BF)
        gv_r[...] = (dg(attn, dh, 0, 0) + fall * dg(kh, rh, 1, 0)).astype(BF)

    tile = pl.BlockSpec((n, w), lambda h: (0, h))
    whole = pl.BlockSpec((n, heads), lambda h: (0, 0))
    state = pl.BlockSpec((1, w, w), lambda h: (h, 0, 0))
    return pl.pallas_call(
        kern,
        grid=(heads,),
        in_specs=[tile] * 4 + [whole, state, state],
        out_specs=[tile] * 4,
        out_shape=[jax.ShapeDtypeStruct(q.shape, BF)] * 4,
        scratch_shapes=[pltpu.VMEM((n, heads), F32)],
        compiler_params=pltpu.CompilerParams(dimension_semantics=("arbitrary",)),
    )(q, k, v, d, ld, s, r)


def parts(x, count):
    out = []
    for _ in range(count):
        p = lax.reduce_precision(x, 8, 7)
        out.append(p.astype(BF))
        x = x - p
    return out


def scan_states(b, c, growth, plan):
    heads, w, _ = b.shape
    here = lax.axis_index("ctx")
    s = r = jnp.zeros((heads, w, w), F32)
    before = after = jnp.ones((heads,), F32)
    total = growth
    wide = lambda a: a[:, None, None]
    bit = 1
    while bit < plan.n_ctx:
        extra = jnp.stack(parts(total, 3)).reshape(1, 3 * heads)
        extra = jnp.pad(extra, ((0, w - 1), (0, w - 3 * heads)))[None]
        got = send(jnp.concatenate([b.astype(BF), c.astype(BF), extra]), plan.block(bit))
        b2, c2 = got[:heads].astype(F32), got[heads : 2 * heads].astype(F32)
        t2 = got[2 * heads, 0, : 3 * heads].astype(F32).reshape(3, heads).sum(axis=0)
        b1, c1 = b.astype(F32), c.astype(F32)
        upper = (here & bit) != 0
        s = jnp.where(upper, s + wide(before) * b2, s)
        r = jnp.where(upper, r, r + wide(after) * c2)
        before = jnp.where(upper, before * t2, before)
        after = jnp.where(upper, after, after * t2)
        b = jnp.where(upper, wide(total) * b2 + b1, wide(t2) * b1 + b2)
        c = jnp.where(upper, c2 + wide(t2) * c1, c1 + wide(total) * c2)
        total = total * t2
        bit *= 2
    return s, r


def expert_half(tokens, first, w_gate, w_up, w_down):
    n = len(tokens)
    rows, wide = tokens[0].shape
    count, hidden, width = w_gate.shape
    fb, db = block_of(hidden, 384), block_of(width, 1024)
    nf, nd = hidden // fb, width // db
    blk = rows
    while blk > 256 and blk % 2 == 0:
        blk //= 2
    cap = blk // 2
    per = rows // blk
    places = [(i, j, i * per + j) for i in range(n) for j in range(per)]
    up_steps = count * nf

    def kern(first_r, *refs):
        tin = refs[:n]
        wg_r, wu_r, wd_r = refs[n : n + 3]
        outs = refs[n + 3 : 2 * n + 3]
        xs, hid, wcol, pt = refs[2 * n + 3 :]
        t = pl.program_id(0)

        def gather(e):
            eid = (first_r[0] + e).astype(F32)
            tri = lax.broadcasted_iota(jnp.int32, (blk, blk), 0) > lax.broadcasted_iota(jnp.int32, (blk, blk), 1)
            slot = lax.broadcasted_iota(jnp.int32, (blk, cap), 1).astype(F32)
            for i, j, b in places:
                side = tin[i][pl.ds(j * blk, blk), width : width + SIDE].astype(F32)
                named = (side[:, 0:1] == eid) | (side[:, 1:2] == eid)
                named = jnp.broadcast_to(named.astype(F32), (blk, cap))
                rank = dg(tri.astype(BF), named.astype(BF), 1, 0)
                member = jnp.where((rank == slot) & (named > 0.0), 1.0, 0.0)
                pt[e, pl.ds(b * blk, blk), :] = member.astype(BF)
                pick = member.T.astype(BF)
                xs[pl.ds(b * cap, cap), :] = dg(pick, tin[i][pl.ds(j * blk, blk), 0:width], 1, 0).astype(BF)
                got = dg(pick, side.astype(BF), 1, 0)
                w0 = got[:, 2:3] + got[:, 3:4] + got[:, 4:5]
                w1 = got[:, 5:6] + got[:, 6:7] + got[:, 7:8]
                scale = jnp.where(got[:, 0:1] == eid, w0, w1)
                wcol[e, pl.ds(b * cap, cap), :] = jnp.broadcast_to(scale, (cap, SIDE))

        for e in range(count):
            for f in range(nf):

                @pl.when(t == e * nf + f)
                def _(e=e, f=f):
                    if f == 0:
                        gather(e)
                    x = xs[...]
                    gate = dg(wg_r[0], x, 1, 1)
                    up = dg(wu_r[0], x, 1, 1)
                    act = gate / (1.0 + jnp.exp(-gate)) * up
                    hid[e, :, f * fb : (f + 1) * fb] = act.T.astype(BF)

        @pl.when(t >= up_steps)
        def _():
            res = [(dg(hid[e], wd_r[e], 1, 0) * wcol[e, :, 0:1]).astype(BF) for e in range(count)]
            for i, j, b in places:
                mix = sum(dg(pt[e, pl.ds(b * blk, blk), :], res[e][b * cap : (b + 1) * cap], 1, 0) for e in range(count))
                outs[i][pl.ds(j * blk, blk), :] = mix.astype(BF)

    def up_map(t, s):
        q = jnp.minimum(t, up_steps - 1)
        return (q // nf, q % nf, 0)

    def down_map(t, s):
        return (0, 0, jnp.maximum(t - up_steps, 0))

    def out_map(t, s):
        return (0, jnp.maximum(t - up_steps, 0))

    held = pl.BlockSpec((rows, wide), lambda t, s: (0, 0), pipeline_mode=pl.Buffered(1))
    slots = len(places) * cap
    return pl.pallas_call(
        kern,
        out_shape=[jax.ShapeDtypeStruct((rows, width), BF)] * n,
        grid_spec=pltpu.PrefetchScalarGridSpec(
            num_scalar_prefetch=1,
            grid=(up_steps + nd,),
            in_specs=[held] * n + [pl.BlockSpec((1, fb, width), up_map)] * 2 + [pl.BlockSpec((count, hidden, db), down_map)],
            out_specs=[pl.BlockSpec((rows, db), out_map)] * n,
            scratch_shapes=[
                pltpu.VMEM((slots, width), BF),
                pltpu.VMEM((count, slots, hidden), BF),
                pltpu.VMEM((count, slots, SIDE), F32),
                pltpu.VMEM((count, len(places) * blk, cap), BF),
            ],
        ),
        compiler_params=pltpu.CompilerParams(dimension_semantics=("arbitrary",), vmem_limit_bytes=58 * 2**20),
    )(first, *tokens, w_gate, w_up, w_down)


def add(a, b):
    return (a.astype(F32) + b.astype(F32)).astype(BF)


def halve(own, other, plan):
    parts_ = (own, other)
    for k in range(plan.stages - 2, -1, -1):
        half = parts_[0].shape[0] // 2
        away = add(parts_[0][half:], parts_[1][half:])
        stay = add(parts_[0][:half], parts_[1][:half])
        parts_ = (stay, send(away, plan.stage(k)))
    return add(*parts_)


def body(queries, attn_keys, attn_values, out_grad, log_decay, moe_input, routes, route_weight, w_gate, w_up, w_down):
    plan = Plan(lax.axis_size("ctx"), lax.axis_size("exp"))
    rows, width = moe_input.shape
    first = (lax.axis_index("exp") * w_gate.shape[0]).astype(jnp.int32).reshape(1)

    cols = [routes[:, 0].astype(BF), routes[:, 1].astype(BF)]
    cols += parts(route_weight[:, 0], 3) + parts(route_weight[:, 1], 3)
    side = jnp.pad(jnp.stack(cols, axis=1), ((0, 0), (0, SIDE - len(cols))))
    near = jnp.concatenate([moe_input, side], axis=1)
    for k in range(plan.stages - 1):
        near = jnp.concatenate([near, send(near, plan.stage(k))], axis=0)
    last = plan.stage(plan.stages - 1)
    far = send(near, last)
    near_mate = send(near, plan.mate())

    b, c = states(queries, attn_keys, attn_values, out_grad, log_decay)
    growth = jnp.exp(jnp.sum(log_decay, axis=0))
    s, r = scan_states(b, c, growth, plan)

    near_own, near_other = expert_half([near, near_mate], first, w_gate, w_up, w_down)
    far_mate = send(far, plan.mate())
    near_back = send(near_other, plan.mate())
    far_own, far_other = expert_half([far, far_mate], first, w_gate, w_up, w_down)
    far_back = send(far_other, plan.mate())
    near_sum = halve(near_own, near_back, plan)
    far_sum = halve(far_own, far_back, plan)
    moe_out = add(near_sum, send(far_sum, last))
    results = finish(queries, attn_keys, attn_values, out_grad, log_decay, s, r)
    return tuple(results) + (moe_out,)


def solution(mesh):
    token = P("ctx", "exp")
    row = P(BOTH, None)
    weight = P("exp", "ctx", None)
    return jax.shard_map(
        body,
        mesh=mesh,
        in_specs=(token,) * 5 + (row,) * 3 + (weight,) * 3,
        out_specs=(token,) * 4 + (row,),
        check_vma=False,
    )
```
